512 devices in a mesh: bucket: 128 (over x, z, core), rerank: 4 (over y).
Axes of the slice: x: 4, y: 4, z: 16, core: 2. Of those that a mesh axis runs over, the one named last changes fastest.
Arguments:
- queries: bfloat16 [32768, 768], P(('bucket', 'rerank')), may hold values from -6 to 6
- class_in: bfloat16 [768, 1024], replicated, may hold values from -0.21875 to 0.21875
- class_out: bfloat16 [1024, 262144], P(None, ('bucket', 'rerank')), may hold values from -0.1875 to 0.1875
- passages: bfloat16 [393216, 768], P(('bucket', 'rerank')), may hold values from -0.19921875 to 0.19921875
- bucket_sizes: int32 [512, 512], P(('bucket', 'rerank')), may hold values from 1 to 8, 768 in all within a row
- bucket_owner: int32 [32768, 8], P(('bucket', 'rerank')), may hold values from 0 to 511, all different within a row; in each aligned block of 64 rows (0 to 63, 64 to 127, ...) at most 2 rows name the same one
- bucket_slot: int32 [32768, 8], P(('bucket', 'rerank')), may hold values from 0 to 511
- embed: bfloat16 [32768, 4096], P('bucket', 'rerank'), may hold values from -6 to 6
- w_gate: bfloat16 [4096, 14336], P('rerank', 'bucket'), may hold values from -0.09375 to 0.09375
- w_up: bfloat16 [4096, 14336], P('rerank', 'bucket'), may hold values from -0.09375 to 0.09375
- w_score: bfloat16 [14336], P('bucket'), may hold values from -0.046875 to 0.046875
- block_tokens: int32 [4, 128], replicated, may hold values from 0 to 32767
Outputs:
- bucket_logit: float32 [32768, 8], P(('bucket', 'rerank'))
- bucket_mass: float32 [32768, 8], P(('bucket', 'rerank'))
- token_scores: float32 [4, 128], P('rerank')
The draws below stay inside these ranges and needn't reach their ends.
Inputs may be any that keep to these rules, and one draw needn't show every extreme that they name: `bucket_owner`: each query names 8 different owner devices, numbered bucket index times the rerank axis's size plus rerank index; within the 64 queries of one device no owner is named more than 2 times, and that many in some devices. `bucket_sizes`: the sizes of one device's 512 buckets sum to 768.
All inputs are finite; a program needn't handle non-finite values.
Results may differ from the reference program's by a relative error of at most 0.0029.
Values may be sent and summed in bfloat16 or wider, within the bound.
A program may use at most 64 MiB of HBM per device.

```python
import math
import jax
import jax.numpy as jnp
import numpy as np
from jax import lax

QD = 768
HID = 1024
BUCK_DEV = 512
PASS_DEV = 768
MOSTB = 8
TOPB = 8
Q_DEV = 64
D = 4096
FF = 14336
VOCAB = 32768
RBLK = 4
TOKB = 128
CAP = 2
Q = 32768
NBUCK = 262144
NPASS = 393216
DEVICES = 512


def touch_ends(drawn, own_key, least, high):
    place = [jax.random.randint(jax.random.fold_in(own_key, axis), (), 0, length) for axis, length in enumerate(drawn.shape)]
    main_axis = drawn.shape.index(max(drawn.shape))
    beside = place[:main_axis] + [(place[main_axis] + 1) % drawn.shape[main_axis]] + place[main_axis + 1:]
    return drawn.at[tuple(place)].set(least).at[tuple(beside)].set(high)


def shard_levels(rng, dims, split, low, high):
    def one(dim, blocks):
        heights = jax.random.uniform(jax.random.fold_in(jax.random.fold_in(rng, 6), dim), (blocks,), jnp.float32, low / len(split), high / len(split))
        return jnp.repeat(jnp.exp(heights), dims[dim] // blocks).reshape((-1,) + (1,) * (len(dims) - dim - 1))

    loudness = one(*split[0])
    for cut in split[1:]:
        loudness = loudness * one(*cut)
    return loudness


def rank_bounds(number_of, skew):
    portions = [(1 << 20) // math.isqrt(standing ** skew) + 1 for standing in range(1, number_of + 1)]
    width = 1 + sum(portions) // (1 << 30)
    return np.cumsum(np.array([max(1, weight // width) for weight in portions]))


def skewed_ids(key, extent, count, skew):
    grid = rank_bounds(count, skew)
    ticket = jax.random.randint(jax.random.fold_in(key, 1), extent, 0, int(grid[count - 1]))
    grade = jnp.searchsorted(jnp.asarray(grid, jnp.int32), ticket, side="right")
    return jax.random.permutation(jax.random.fold_in(key, 2), count)[grade].astype(jnp.int32)


def length_profile(amount, total, bound, lean):
    weights = [(1 << 20) // math.isqrt(grade ** lean) + 1 for grade in range(2, amount + 1)]
    rest, counts = total - bound - (amount - 1), [1] * (amount - 1)
    while rest > 0:
        candidates = [i for i in range(amount - 1) if counts[i] < bound]
        whole, left = sum([weights[i] for i in candidates]), rest
        for i in candidates:
            more = min(bound - counts[i], max(1, left * weights[i] // whole), rest)
            counts[i] = counts[i] + more
            rest = rest - more
    return np.array([bound] + counts)


def uneven_parts(rng, amount, total, limit, slope):
    if amount == 2:
        one = jax.random.randint(rng, (), max(1, total - limit), min(limit, total - 1) + 1)
        return jnp.stack([one, total - one])
    sizes = jnp.asarray(length_profile(amount, total, limit, slope), jnp.int32)
    twos = (amount - 1) // 2
    source_of, taker = sizes[1:1 + 2 * twos:2], sizes[2:2 + 2 * twos:2]
    margin = jnp.minimum(source_of - 1, limit - taker)
    passed = jax.random.randint(jax.random.fold_in(rng, 1), (twos,), 0, 1 << 20) % (margin + 1)
    sizes = sizes.at[1:1 + 2 * twos:2].set(source_of - passed).at[2:2 + 2 * twos:2].set(taker + passed)
    return sizes[jax.random.permutation(jax.random.fold_in(rng, 2), amount)]


def shared_out(key, own, number, rows, number_of, top, most, skew):
    order = jax.random.permutation(key, number_of)
    heavy_load, usual = load_shares(number_of, rows * top, most, skew, True), load_shares(number_of, rows * top, most, skew, False)
    places = jnp.arange(number_of)

    def named(tallies, turn):
        used = int((tallies > 0).sum())
        fixed = max(1, used // 4)
        passed = fixed + (places - fixed + turn * (used - fixed)) % max(1, number_of - fixed)
        return jnp.zeros((number_of,), jnp.int32).at[order[jnp.where(places < fixed, places, passed)]].set(jnp.asarray(tallies, jnp.int32))

    tallies = jnp.where(number % 4 == 0, named(heavy_load, number // 4), named(usual, number - number // 4 - 1))
    mixed = jax.random.permutation(jax.random.fold_in(own, 3), number_of)
    giver, taker = mixed[0:number_of // 2 * 2:2], mixed[1:number_of // 2 * 2:2]
    room = jnp.minimum(tallies[giver] - 1, most - tallies[taker]) // 2
    room = jnp.where((giver == order[0]) | (taker == order[0]) | (tallies[taker] == 0), 0, jnp.maximum(room, 0))
    passed = jax.random.randint(jax.random.fold_in(own, 4), (number_of // 2,), 0, 1 << 20) % (room + 1)
    tallies = tallies.at[giver].add(-passed).at[taker].add(passed)
    items = jnp.searchsorted(jnp.cumsum(tallies), jnp.arange(rows * top), side="right").astype(jnp.int32)
    grid = items.reshape(top, rows).T
    grid = grid[jax.random.permutation(jax.random.fold_in(own, 1), rows)]
    turn = jax.random.randint(jax.random.fold_in(own, 2), (rows, 1), 0, top)
    return jnp.take_along_axis(grid, (jnp.arange(top)[None, :] + turn) % top, axis=1)


def load_shares(amount, total, bound, lean, full):
    weights = [(1 << 20) // math.isqrt(grade ** lean) + 1 for grade in range(1, amount + 1)]
    largest = bound if full else min(bound, max(-(-total // amount), total * weights[0] // sum(weights)))
    least = 1 if total - largest >= amount - 1 else 0
    holding, rest = [largest] + [least] * (amount - 1), total - largest - least * (amount - 1)
    while rest > 0:
        movable = [i for i in range(1, amount) if holding[i] < largest] or [i for i in range(1, amount) if holding[i] < bound]
        whole, budget = sum([weights[i] for i in movable]), rest
        for i in movable:
            extra = min(bound - holding[i], max(1, budget * weights[i] // whole), rest)
            holding[i] = holding[i] + extra
            rest = rest - extra
    return np.array(holding)


def gaussian(own_key, shape, scale, reach, pieces=(), kind=jnp.bfloat16):
    level = shard_levels(own_key, shape, pieces, -0.22, 0.18) if pieces else 1.0
    entries = jax.random.normal(own_key, shape, jnp.float32) * scale * level
    return jnp.minimum(jnp.maximum(entries, -reach), reach).astype(kind)


def setup_inputs(seed: int = 0) -> dict:
    key_of = jax.random.split(jax.random.key(seed), 13)
    queries = gaussian(key_of[0], (Q, QD), 1.0, 6.0, ((0, 512),))
    class_in = gaussian(key_of[1], (QD, HID), QD ** -0.5, 0.21875)
    class_out = gaussian(key_of[2], (HID, NBUCK), HID ** -0.5, 0.1875, ((1, 512),))
    passages = gaussian(key_of[3], (NPASS, QD), 0.036, 0.19921875, ((0, 512),))
    bucket_sizes = jax.vmap(lambda own: uneven_parts(own, BUCK_DEV, PASS_DEV, MOSTB, 1))(jax.random.split(key_of[4], DEVICES)).reshape((DEVICES, BUCK_DEV)).astype(jnp.int32)
    bucket_owner_keys = jax.random.split(jax.random.fold_in(key_of[5], 1), Q // Q_DEV)
    bucket_owner_turns = jax.random.permutation(jax.random.fold_in(key_of[5], 3), Q // Q_DEV)
    bucket_owner = jax.vmap(lambda own, number: shared_out(jax.random.fold_in(key_of[5], 2), own, number, Q_DEV, DEVICES, TOPB, CAP, 2))(bucket_owner_keys, bucket_owner_turns).reshape((Q, TOPB))
    bucket_slot = touch_ends(jax.random.randint(key_of[6], (Q, TOPB), 0, BUCK_DEV), jax.random.fold_in(key_of[6], 1), 0, BUCK_DEV - 1).astype(jnp.int32)
    embed = gaussian(key_of[7], (VOCAB, D), 1.0, 6.0, ((0, 128), (1, 4)))
    w_gate = gaussian(key_of[8], (D, FF), D ** -0.5, 0.09375, ((0, 4), (1, 128)))
    w_up = gaussian(key_of[9], (D, FF), D ** -0.5, 0.09375, ((0, 4), (1, 128)))
    w_score = gaussian(key_of[10], (FF,), FF ** -0.5, 0.046875, ((0, 128),))
    block_tokens = touch_ends(skewed_ids(key_of[11], (RBLK, TOKB), VOCAB, 2), jax.random.fold_in(key_of[11], 3), 0, VOCAB - 1).astype(jnp.int32)
    return {"queries": queries, "class_in": class_in, "class_out": class_out, "passages": passages, "bucket_sizes": bucket_sizes, "bucket_owner": bucket_owner, "bucket_slot": bucket_slot, "embed": embed, "w_gate": w_gate, "w_up": w_up, "w_score": w_score, "block_tokens": block_tokens}


def reference(queries, class_in, class_out, passages, bucket_sizes, bucket_owner, bucket_slot, embed, w_gate, w_up, w_score, block_tokens):
    hidden = jax.nn.relu(jnp.dot(queries, class_in, preferred_element_type=jnp.float32)).astype(jnp.bfloat16)
    bucket_end = jnp.cumsum(bucket_sizes, axis=1).astype(jnp.int32)
    bucket_start = (bucket_end - bucket_sizes).astype(jnp.int32)
    owner_ids = bucket_owner.astype(jnp.int32)
    slot_ids = bucket_slot.astype(jnp.int32)
    first_row = (owner_ids * PASS_DEV + bucket_start[owner_ids, slot_ids]).astype(jnp.int32)
    row_count = bucket_sizes[owner_ids, slot_ids].astype(jnp.int32)
    chosen_column = (owner_ids * BUCK_DEV + slot_ids).astype(jnp.int32)
    block_rows = math.gcd(Q, 512)

    def one_block(items):
        hidden_block, query_block, column_block, first_block, count_block = items
        picked_cols = jnp.take(class_out, column_block, axis=1).astype(jnp.float32)
        slot_logit = jnp.einsum("hqk,qh->qk", picked_cols, hidden_block.astype(jnp.float32))
        slot_mass = jnp.zeros(column_block.shape, jnp.float32)
        for step in range(MOSTB):
            picked = jnp.take(passages, jnp.minimum(first_block + step, NPASS - 1), axis=0).astype(jnp.float32)
            similar = jnp.einsum("qkd,qd->qk", picked, query_block.astype(jnp.float32))
            slot_mass = slot_mass + jnp.where(step < count_block, jnp.exp(similar), jnp.float32(0.0))
        return slot_logit, slot_mass

    def blocked(array):
        return array.reshape((Q // block_rows, block_rows) + array.shape[1:])

    slot_logit, slot_mass = lax.map(one_block, (blocked(hidden), blocked(queries), blocked(chosen_column), blocked(first_row), blocked(row_count)))
    bucket_logit = slot_logit.reshape(Q, TOPB)
    bucket_mass = slot_mass.reshape(Q, TOPB)

    tokens = block_tokens.reshape(-1).astype(jnp.int32)
    token_rows = jnp.take(embed, tokens, axis=0)
    gate_full = jnp.dot(token_rows, w_gate, preferred_element_type=jnp.float32)
    up_full = jnp.dot(token_rows, w_up, preferred_element_type=jnp.float32)
    mixed_rows = jax.nn.silu(gate_full) * up_full
    scores = jnp.dot(mixed_rows, w_score.astype(jnp.float32), precision=lax.Precision.HIGHEST)
    token_scores = scores.reshape(RBLK, TOKB)
    return bucket_logit, bucket_mass, token_scores
```

```python
import functools

import jax
import jax.numpy as jnp
from jax import lax
from jax.experimental import pallas as pl
from jax.experimental.pallas import tpu as pltpu
from jax.sharding import Mesh, PartitionSpec as P

AXES = ("x", "z", "c", "y")
NX, NZ, NC, NY = 4, 16, 2, 4
NO = NX * NC * NY
BF = jnp.bfloat16
F32 = jnp.float32
VM = pl.BlockSpec(memory_space=pltpu.VMEM)


def here():
    return tuple(lax.axis_index(a) for a in AXES)


def remote(src, dst, send, recv, device):
    return pltpu.make_async_remote_copy(
        src_ref=src,
        dst_ref=dst,
        send_sem=send,
        recv_sem=recv,
        device_id=device,
        device_id_type=pl.DeviceIdType.MESH,
    )


def greet(peers_of, count):
    barrier = pltpu.get_barrier_semaphore()

    @pl.loop(1, count)
    def _(k):
        device, _ = peers_of(k)
        pl.semaphore_signal(barrier, inc=1, device_id=device, device_id_type=pl.DeviceIdType.MESH)


def plane_peer(k):
    x, z, c, y = here()
    px = lax.rem(x + k // (NC * NY), NX)
    pc = lax.rem(c + lax.rem(k // NY, NC), NC)
    py = lax.rem(y + lax.rem(k, NY), NY)
    return (px, z, pc, py), (px * NC + pc) * NY + py


def side_peer(k):
    x, z, c, y = here()
    px = lax.rem(x + k // NC, NX)
    pc = lax.rem(c + lax.rem(k, NC), NC)
    return (px, z, pc, y), px * NC + pc


def line_peer(k):
    x, z, c, y = here()
    pz = lax.rem(z + k, NZ)
    return (x, pz, c, y), pz


def row_peer(k):
    x, z, c, y = here()
    py = lax.rem(y + k, NY)
    return (x, z, c, py), py


def line_gather(q_ref, i_ref, out_ref, iout_ref, send_sem, recv_sem):
    x, z, c, y = here()
    right = (x, lax.rem(z + 1, NZ), c, y)
    left = (x, lax.rem(z + NZ - 1, NZ), c, y)
    barrier = pltpu.get_barrier_semaphore()
    for device in (left, right):
        pl.semaphore_signal(barrier, inc=1, device_id=device, device_id_type=pl.DeviceIdType.MESH)
    pl.semaphore_wait(barrier, 2)

    def copy(way, step, part):
        place = lax.rem(z + (NZ - step if way == 0 else step), NZ)
        device = right if way == 0 else left
        if part < 2:
            src = q_ref.at[part] if step == 0 else out_ref.at[place, part]
            dst = out_ref.at[place, part]
        else:
            src = i_ref if step == 0 else iout_ref.at[place]
            dst = iout_ref.at[place]
        return remote(src, dst, send_sem.at[way, step, part], recv_sem.at[way, step, part], device)

    started = {}
    for step in range(NZ // 2):
        for part in (2, 0, 1):
            for way in (0, 1):
                if step > 0 and (way, step - 1, part) in started:
                    started[way, step - 1, part].wait_recv()
                if way == 1 and step == NZ // 2 - 1:
                    continue
                started[way, step, part] = copy(way, step, part)
                started[way, step, part].start()
        if step == 0:
            out_ref[z] = q_ref[...]
            iout_ref[z] = i_ref[...]
    for (way, step, part), done in started.items():
        if way == 0 and step == NZ // 2 - 1:
            done.wait_recv()
        done.wait_send()


def gather_line(rows, ints):
    return pl.pallas_call(
        line_gather,
        out_shape=(
            jax.ShapeDtypeStruct((NZ,) + rows.shape, rows.dtype),
            jax.ShapeDtypeStruct((NZ,) + ints.shape, ints.dtype),
        ),
        in_specs=[VM, VM],
        out_specs=(VM, VM),
        scratch_shapes=[
            pltpu.SemaphoreType.DMA((2, NZ // 2, 3)),
            pltpu.SemaphoreType.DMA((2, NZ // 2, 3)),
        ],
        compiler_params=pltpu.CompilerParams(collective_id=0, has_side_effects=True),
    )(rows, ints)


def exchange_kernel(q_ref, s_ref, out_ref, sout_ref, send_sem, recv_sem, ssend, srecv):
    _, me = plane_peer(0)
    greet(plane_peer, NO)
    pl.semaphore_wait(pltpu.get_barrier_semaphore(), NO - 1)

    def copies(k):
        device, place = plane_peer(k)
        return (
            remote(q_ref.at[place], out_ref.at[me], send_sem.at[k], recv_sem.at[k], device),
            remote(s_ref.at[place], sout_ref.at[me], ssend.at[k], srecv.at[k], device),
        )

    @pl.loop(1, NO)
    def _(k):
        for each in copies(k):
            each.start()

    out_ref[me] = q_ref[me]
    sout_ref[me] = s_ref[me]

    @pl.loop(1, NO)
    def _(k):
        for each in copies(k):
            each.wait()


def exchange(rows, slots):
    return pl.pallas_call(
        exchange_kernel,
        out_shape=(
            jax.ShapeDtypeStruct(rows.shape, rows.dtype),
            jax.ShapeDtypeStruct(slots.shape, slots.dtype),
        ),
        in_specs=[VM, VM],
        out_specs=(VM, VM),
        scratch_shapes=[pltpu.SemaphoreType.DMA((NO,)) for _ in range(4)],
        compiler_params=pltpu.CompilerParams(collective_id=1, has_side_effects=True),
    )(rows, slots)


def token_kernel(
    picks_ref, embed_ref, w_ref, ws_ref, out_ref,
    p1, r1, s2, r2, s3, r3, r4, rows, gu, r5,
    ss1, rs1, ss2, rs2, ss3, rs3, ss4, rs4, ss5, rs5,
):
    ns = NX * NC
    _, me = side_peer(0)
    _, z, _, y = here()
    greet(side_peer, ns)
    greet(line_peer, NZ)
    greet(row_peer, NY)
    pl.semaphore_wait(pltpu.get_barrier_semaphore(), ns + NZ + NY - 3)

    def partial(place):
        part = jnp.dot(picks_ref[place], embed_ref[...], preferred_element_type=F32).astype(BF)
        for f in range(8):
            for h in range(2):
                p1[place, 2 * f + h] = part[h * 32 : h * 32 + 32, f * 128 : f * 128 + 128]

    def first(k):
        device, place = side_peer(k)
        return remote(p1.at[place], r1.at[me], ss1.at[k], rs1.at[k], device)

    @pl.loop(1, ns)
    def _(k):
        _, place = side_peer(k)
        partial(place)
        first(k).start()

    partial(me)
    r1[me] = p1[me]

    @pl.loop(1, ns)
    def _(k):
        first(k).wait()

    total = r1[0]
    for j in range(1, ns):
        total = total + r1[j]
    s2[...] = total

    def second(k):
        device, place = line_peer(k)
        return remote(s2.at[place], r2.at[z], ss2.at[k], rs2.at[k], device)

    @pl.loop(1, NZ)
    def _(k):
        second(k).start()

    r2[z] = s2[z]

    @pl.loop(1, NZ)
    def _(k):
        second(k).wait()

    total = r2[0]
    for j in range(1, NZ):
        total = total + r2[j]
    s3[...] = total

    def third(k):
        device, place = line_peer(k)
        return remote(s3, r3.at[z], ss3.at[k], rs3.at[k], device)

    @pl.loop(1, NZ)
    def _(k):
        third(k).start()

    r3[z] = s3[...]

    @pl.loop(1, NZ)
    def _(k):
        third(k).wait()

    def fourth(k):
        device, place = side_peer(k)
        return remote(r3, r4.at[me], ss4.at[k], rs4.at[k], device)

    @pl.loop(1, ns)
    def _(k):
        fourth(k).start()

    r4[me] = r3[...]

    @pl.loop(1, ns)
    def _(k):
        fourth(k).wait()

    for j in range(ns):
        for f in range(8):
            for h in range(2):
                at = j * 64 + h * 32
                rows[at : at + 32, f * 128 : f * 128 + 128] = r4[j, 2 * f + h]

    def fifth(k):
        device, place = row_peer(k)
        return remote(gu.at[place], r5.at[y], ss5.at[k], rs5.at[k], device)

    def project(place):
        block = rows[pl.ds(pl.multiple_of(place * 128, 128), 128), :]
        gu[place] = jnp.dot(block, w_ref[...], preferred_element_type=F32)

    @pl.loop(1, NY)
    def _(k):
        _, place = row_peer(k)
        project(place)
        fifth(k).start()

    project(y)
    r5[y] = gu[y]

    @pl.loop(1, NY)
    def _(k):
        fifth(k).wait()

    both = (r5[0] + r5[1]) + (r5[2] + r5[3])
    gate, up = both[:, :128], both[:, 128:]
    mixed = gate / (1.0 + jnp.exp(-gate)) * up
    score = lax.dot_general(
        ws_ref[...],
        mixed,
        (((1,), (1,)), ((), ())),
        precision=lax.Precision.HIGHEST,
        preferred_element_type=F32,
    )
    out_ref[...] = score


def token_part(picks, embed, w, ws):
    ns = NX * NC
    dma = pltpu.SemaphoreType.DMA
    return pl.pallas_call(
        token_kernel,
        out_shape=jax.ShapeDtypeStruct((8, 128), F32),
        in_specs=[VM] * 4,
        out_specs=VM,
        scratch_shapes=[
            pltpu.VMEM((ns, NZ, 32, 128), BF),
            pltpu.VMEM((ns, NZ, 32, 128), BF),
            pltpu.VMEM((NZ, 32, 128), BF),
            pltpu.VMEM((NZ, 32, 128), BF),
            pltpu.VMEM((32, 128), BF),
            pltpu.VMEM((NZ, 32, 128), BF),
            pltpu.VMEM((ns, NZ, 32, 128), BF),
            pltpu.VMEM((512, 1024), BF),
            pltpu.VMEM((NY, 128, 256), F32),
            pltpu.VMEM((NY, 128, 256), F32),
            dma((ns,)), dma((ns,)), dma((NZ,)), dma((NZ,)), dma((NZ,)),
            dma((NZ,)), dma((ns,)), dma((ns,)), dma((NY,)), dma((NY,)),
        ],
        compiler_params=pltpu.CompilerParams(collective_id=2, has_side_effects=True),
    )(picks, embed, w, ws)


def return_kernel(
    ret_ref, score_ref, table_ref, out_ref, r1, s2, c1, d2, c2,
    ss1, rs1, cs1, cr1, ss2, rs2, cs2, cr2,
):
    ns = NX * NC
    _, me = plane_peer(0)
    _, side = side_peer(0)
    _, z, _, _ = here()
    greet(plane_peer, NO)
    greet(line_peer, NZ)
    pl.semaphore_wait(pltpu.get_barrier_semaphore(), NO + NZ - 2)

    def back(k):
        device, place = plane_peer(k)
        return remote(ret_ref.at[place], r1.at[me], ss1.at[k], rs1.at[k], device)

    def score1(k):
        device, _ = side_peer(k)
        return remote(score_ref, c1.at[side], cs1.at[k], cr1.at[k], device)

    @pl.loop(1, NO)
    def _(k):
        back(k).start()

    @pl.loop(1, ns)
    def _(k):
        score1(k).start()

    r1[me] = ret_ref[me]
    c1[side] = score_ref[...]

    @pl.loop(1, NO)
    def _(k):
        back(k).wait()

    @pl.loop(1, ns)
    def _(k):
        score1(k).wait()

    total = r1[0]
    for j in range(1, NO):
        total = total + r1[j]
    s2[...] = total
    total = c1[0]
    for j in range(1, ns):
        total = total + c1[j]
    d2[...] = total

    def line(k):
        device, place = line_peer(k)
        return (
            remote(s2.at[place], table_ref.at[z], ss2.at[k], rs2.at[k], device),
            remote(d2, c2.at[z], cs2.at[k], cr2.at[k], device),
        )

    @pl.loop(1, NZ)
    def _(k):
        for each in line(k):
            each.start()

    table_ref[z] = s2[z]
    c2[z] = d2[...]

    @pl.loop(1, NZ)
    def _(k):
        for each in line(k):
            each.wait()

    total = c2[0]
    for j in range(1, NZ):
        total = total + c2[j]
    out_ref[...] = total


def give_back(ret, score):
    ns = NX * NC
    dma = pltpu.SemaphoreType.DMA
    return pl.pallas_call(
        return_kernel,
        out_shape=(
            jax.ShapeDtypeStruct((NZ, 1, 128), F32),
            jax.ShapeDtypeStruct((1, 128), F32),
        ),
        in_specs=[VM, VM],
        out_specs=(VM, VM),
        scratch_shapes=[
            pltpu.VMEM((NO, NZ, 1, 128), F32),
            pltpu.VMEM((NZ, 1, 128), F32),
            pltpu.VMEM((ns, 1, 128), F32),
            pltpu.VMEM((1, 128), F32),
            pltpu.VMEM((NZ, 1, 128), F32),
            dma((NO,)), dma((NO,)), dma((ns,)), dma((ns,)),
            dma((NZ,)), dma((NZ,)), dma((NZ,)), dma((NZ,)),
        ],
        compiler_params=pltpu.CompilerParams(collective_id=3, has_side_effects=True),
    )(ret, score)


def body(
    queries,
    class_in,
    class_out,
    passages,
    bucket_sizes,
    bucket_owner,
    bucket_slot,
    embed,
    w_gate,
    w_up,
    w_score,
    block_tokens,
):
    x, z, c, y = here()
    mine = (x * NC + c) * NY + y
    rows, top = bucket_owner.shape
    width = queries.shape[1]
    i32 = jnp.int32

    owner_flat = bucket_owner.reshape(rows * top)
    order = jnp.arange(rows * top, dtype=i32)
    earlier = (owner_flat[:, None] == owner_flat[None, :]) & (order[None, :] < order[:, None])
    rank = jnp.sum(earlier.astype(i32), axis=1).reshape(rows, top)
    own_y = bucket_owner % NY
    own_c = (bucket_owner // NY) % NC
    own_z = (bucket_owner // (NY * NC)) % NZ
    own_x = bucket_owner // (NY * NC * NZ)
    own_o = (own_x * NC + own_c) * NY + own_y
    code = (own_z * NO + own_o) * 2 + rank
    ints = jnp.concatenate([code.T, bucket_slot.T + 1], axis=0)
    ints = jnp.pad(ints, ((0, 0), (0, 128 - rows)))

    line_rows, line_ints = gather_line(queries.reshape(2, rows // 2, width), ints)
    line_rows = line_rows.reshape(NZ * rows, width)
    line_code = line_ints[:, :top, :rows].transpose(1, 0, 2).reshape(top, NZ * rows)
    line_slot = line_ints[:, top : 2 * top, :rows].transpose(1, 0, 2).reshape(top, NZ * rows)
    wanted = z * NO + jnp.arange(NO, dtype=i32)
    hit = (line_code // 2)[None, :, :] == wanted[:, None, None]
    turn = jnp.sum(jnp.where(hit, line_code[None] % 2 + 1, 0), axis=1)
    slot_of = jnp.sum(jnp.where(hit, line_slot[None], 0), axis=1)
    place = jnp.arange(NZ * 2, dtype=i32)
    col = jnp.arange(NZ * rows, dtype=i32)
    chosen = (turn[:, None, :] == (place % 2 + 1)[None, :, None]) & (
        (place // 2)[:, None] == (col // rows)[None, :]
    )[None]
    send_slots = jnp.sum(jnp.where(chosen, slot_of[:, None, :], 0), axis=2)
    send_rows = jnp.dot(
        chosen.astype(BF).reshape(NO * NZ * 2, NZ * rows), line_rows, preferred_element_type=F32
    ).astype(BF)
    send_slots = jnp.pad(send_slots, ((0, 0), (0, 128 - 2 * NZ))).reshape(NO, 1, 128)
    got_rows, got_slots = exchange(send_rows.reshape(NO, NZ * 2, width), send_slots)
    got_rows = got_rows.reshape(NO * NZ * 2, width)
    got_slots = got_slots.reshape(NO, 128)[:, : 2 * NZ].reshape(NO * NZ * 2) - 1

    hidden = jax.nn.relu(jnp.dot(got_rows, class_in, preferred_element_type=F32)).astype(BF)
    all_logits = jnp.dot(hidden, class_out, preferred_element_type=F32)
    columns = jnp.arange(class_out.shape[1], dtype=i32)
    slot_logit = jnp.sum(jnp.where(got_slots[:, None] == columns[None, :], all_logits, 0.0), axis=1)
    bucket_end = jnp.cumsum(bucket_sizes.reshape(-1))
    positions = jnp.arange(passages.shape[0], dtype=i32)
    passage_bucket = jnp.sum((bucket_end[:, None] <= positions[None, :]).astype(i32), axis=0)
    similar = jnp.einsum("sd,pd->sp", got_rows, passages, preferred_element_type=F32)
    slot_mass = jnp.sum(
        jnp.where(got_slots[:, None] == passage_bucket[None, :], jnp.exp(similar), 0.0), axis=1
    )
    lane = jnp.arange(128, dtype=i32)
    logit3 = slot_logit.reshape(NO, NZ, 2)
    mass3 = slot_mass.reshape(NO, NZ, 2)
    odd = lane % 2 == 1
    spread = jnp.where(
        lane < 64,
        jnp.where(odd, logit3[:, :, 1:], logit3[:, :, :1]),
        jnp.where(odd, mass3[:, :, 1:], mass3[:, :, :1]),
    )
    ret = jnp.where((lane % 64) // 2 == mine, spread, 0.0).reshape(NO, NZ, 1, 128)

    vocab_rows = embed.shape[0]
    local_ids = block_tokens.reshape(-1) - ((x * NZ + z) * NC + c) * vocab_rows
    picks = (local_ids[:, None] == jnp.arange(vocab_rows, dtype=i32)[None, :]).astype(BF)
    fill = 128 - w_gate.shape[1]
    w = jnp.concatenate(
        [jnp.pad(w_gate, ((0, 0), (0, fill))), jnp.pad(w_up, ((0, 0), (0, fill)))], axis=1
    )
    ws = jnp.broadcast_to(jnp.pad(w_score.astype(F32), (0, fill))[None, :], (8, 128))
    score = token_part(picks.reshape(NX * NC, 64, vocab_rows), embed, w, ws)

    table, token_scores = give_back(ret, score[:1])
    table = table.reshape(NZ, 128)
    logit_table = table[:, :64].reshape(NZ * 64)
    mass_table = table[:, 64:].reshape(NZ * 64)
    pick = code.reshape(-1)[:, None] == jnp.arange(NZ * 64, dtype=i32)[None, :]
    bucket_logit = jnp.sum(jnp.where(pick, logit_table[None], 0.0), axis=1).reshape(rows, top)
    bucket_mass = jnp.sum(jnp.where(pick, mass_table[None], 0.0), axis=1).reshape(rows, top)
    return (bucket_logit, bucket_mass, token_scores)


def solution(mesh):
    fine = Mesh(mesh.devices.reshape(NX, NZ, NC, NY), AXES)
    group = ("x", "z", "c")
    placed = (
        P(AXES, None),
        P(),
        P(None, AXES),
        P(AXES, None),
        P(AXES, None),
        P(AXES, None),
        P(AXES, None),
        P(group, "y"),
        P("y", group),
        P("y", group),
        P(group),
        P(),
    )
    return jax.shard_map(
        body,
        mesh=fine,
        in_specs=placed,
        out_specs=(P(AXES, None), P(AXES, None), P("y", None)),
        check_vma=False,
    )
```

```python
import jax
import jax.numpy as jnp
from jax import lax
from jax.experimental import pallas as pl
from jax.experimental.pallas import tpu as pltpu
from jax.sharding import Mesh, PartitionSpec as P

AXES = ("x", "z", "c", "y")
NX, NZ, NC, NY = 4, 16, 2, 4
NO = NX * NC * NY
BF = jnp.bfloat16
F32 = jnp.float32
VM = pl.BlockSpec(memory_space=pltpu.VMEM)


def here():
    return tuple(lax.axis_index(a) for a in AXES)


def remote(src, dst, send, recv, device):
    return pltpu.make_async_remote_copy(
        src_ref=src,
        dst_ref=dst,
        send_sem=send,
        recv_sem=recv,
        device_id=device,
        device_id_type=pl.DeviceIdType.MESH,
    )


def greet(peers_of, count):
    barrier = pltpu.get_barrier_semaphore()

    @pl.loop(1, count)
    def _(k):
        device, _ = peers_of(k)
        pl.semaphore_signal(barrier, inc=1, device_id=device, device_id_type=pl.DeviceIdType.MESH)


def plane_peer(k):
    x, z, c, y = here()
    px = lax.rem(x + k // (NC * NY), NX)
    pc = lax.rem(c + lax.rem(k // NY, NC), NC)
    py = lax.rem(y + lax.rem(k, NY), NY)
    return (px, z, pc, py), (px * NC + pc) * NY + py


def side_peer(k):
    x, z, c, y = here()
    px = lax.rem(x + k // NC, NX)
    pc = lax.rem(c + lax.rem(k, NC), NC)
    return (px, z, pc, y), px * NC + pc


def line_peer(k):
    x, z, c, y = here()
    pz = lax.rem(z + k, NZ)
    return (x, pz, c, y), pz


def row_peer(k):
    x, z, c, y = here()
    py = lax.rem(y + k, NY)
    return (x, z, c, py), py


def line_kernel(
    q_ref, i_ref, picks_ref, embed_ref, out_ref, iout_ref, r3_ref,
    p1, r1, s2, r2, s3, send_sem, recv_sem, ss1, rs1, ss2, rs2, ss3, rs3,
):
    ns = NX * NC
    x, z, c, y = here()
    _, me = side_peer(0)
    right = (x, lax.rem(z + 1, NZ), c, y)
    left = (x, lax.rem(z + NZ - 1, NZ), c, y)
    greet(line_peer, NZ)
    greet(side_peer, ns)
    pl.semaphore_wait(pltpu.get_barrier_semaphore(), NZ + ns - 2)

    def copy(way, step, part):
        place = lax.rem(z + (NZ - step if way == 0 else step), NZ)
        device = right if way == 0 else left
        if part < 2:
            src = q_ref.at[part] if step == 0 else out_ref.at[place, part]
            dst = out_ref.at[place, part]
        else:
            src = i_ref if step == 0 else iout_ref.at[place]
            dst = iout_ref.at[place]
        return remote(src, dst, send_sem.at[way, step, part], recv_sem.at[way, step, part], device)

    def partial(place):
        part = jnp.dot(picks_ref[place], embed_ref[...], preferred_element_type=F32).astype(BF)
        for f in range(8):
            for h in range(2):
                p1[place, 2 * f + h] = part[h * 32 : h * 32 + 32, f * 128 : f * 128 + 128]

    def first(k):
        device, place = side_peer(k)
        return remote(p1.at[place], r1.at[me], ss1.at[k], rs1.at[k], device)

    def second(k):
        device, place = line_peer(k)
        return remote(s2.at[place], r2.at[z], ss2.at[k], rs2.at[k], device)

    def third(k):
        device, _ = line_peer(k)
        return remote(s3, r3_ref.at[z], ss3.at[k], rs3.at[k], device)

    def start_second():
        @pl.loop(1, ns)
        def _(k):
            first(k).wait()

        total = r1[0]
        for j in range(1, ns):
            total = total + r1[j]
        s2[...] = total

        @pl.loop(1, NZ)
        def _(k):
            second(k).start()

        r2[z] = s2[z]

    def start_third():
        @pl.loop(1, NZ)
        def _(k):
            second(k).wait()

        total = r2[0]
        for j in range(1, NZ):
            total = total + r2[j]
        s3[...] = total

        @pl.loop(1, NZ)
        def _(k):
            third(k).start()

        r3_ref[z] = s3[...]

    started = {}
    for step in range(NZ // 2):
        for part in (2, 0, 1):
            for way in (0, 1):
                if step > 0 and (way, step - 1, part) in started:
                    started[way, step - 1, part].wait_recv()
                if way == 1 and step == NZ // 2 - 1:
                    continue
                started[way, step, part] = copy(way, step, part)
                started[way, step, part].start()
        if step < 4:

            @pl.loop(1 + 2 * step, min(3 + 2 * step, ns))
            def _(k):
                _, place = side_peer(k)
                partial(place)
                first(k).start()

        if step == 3:
            partial(me)
            r1[me] = p1[me]
            out_ref[z] = q_ref[...]
            iout_ref[z] = i_ref[...]
        if step == 5:
            start_second()
    start_third()
    for (way, step, part), done in started.items():
        if way == 0 and step == NZ // 2 - 1:
            done.wait_recv()
        done.wait_send()

    @pl.loop(1, NZ)
    def _(k):
        third(k).wait()


def gather_line(rows, ints, picks, embed):
    ns = NX * NC
    dma = pltpu.SemaphoreType.DMA
    return pl.pallas_call(
        line_kernel,
        out_shape=(
            jax.ShapeDtypeStruct((NZ,) + rows.shape, rows.dtype),
            jax.ShapeDtypeStruct((NZ,) + ints.shape, ints.dtype),
            jax.ShapeDtypeStruct((NZ, 32, 128), BF),
        ),
        in_specs=[VM] * 4,
        out_specs=(VM, VM, VM),
        scratch_shapes=[
            pltpu.VMEM((ns, NZ, 32, 128), BF),
            pltpu.VMEM((ns, NZ, 32, 128), BF),
            pltpu.VMEM((NZ, 32, 128), BF),
            pltpu.VMEM((NZ, 32, 128), BF),
            pltpu.VMEM((32, 128), BF),
            dma((2, NZ // 2, 3)), dma((2, NZ // 2, 3)),
            dma((ns,)), dma((ns,)), dma((NZ,)), dma((NZ,)), dma((NZ,)), dma((NZ,)),
        ],
        compiler_params=pltpu.CompilerParams(collective_id=0, has_side_effects=True),
    )(rows, ints, picks, embed)


def exchange_kernel(
    q_ref, s_ref, r3_ref, w_ref, ws_ref, out_ref, sout_ref, score_ref,
    r4, rows, gu, r5, send_sem, recv_sem, ssend, srecv, ss4, rs4, sc4, rc4, ss5, rs5,
):
    x, z, c, y = here()
    ns = NX * NC
    _, me = plane_peer(0)
    greet(plane_peer, NO)
    pl.semaphore_wait(pltpu.get_barrier_semaphore(), NO - 1)
    partner = (x, z, 1 - c, y)

    def along_x(k):
        device = (lax.rem(x + k, NX), z, c, y)
        return remote(r3_ref, r4.at[x * NC + c], ss4.at[k], rs4.at[k], device)

    def across(k):
        place = lax.rem(x + NX - k, NX) * NC + c
        return remote(r4.at[place], r4.at[place], sc4.at[k], rc4.at[k], partner)

    def copies(k):
        device, place = plane_peer(k)
        return (
            remote(q_ref.at[place], out_ref.at[me], send_sem.at[k], recv_sem.at[k], device),
            remote(s_ref.at[place], sout_ref.at[me], ssend.at[k], srecv.at[k], device),
        )

    for k in (2, 1, 3):
        along_x(k).start()
    r4[x * NC + c] = r3_ref[...]
    across(0).start()

    @pl.loop(1, NO)
    def _(k):
        for each in copies(k):
            each.start()

    out_ref[me] = q_ref[me]
    sout_ref[me] = s_ref[me]

    for k in (1, 3, 2):
        along_x(k).wait_recv()
        across(k).start()
    for k in range(NX):
        across(k).wait_recv()

    for j in range(ns):
        for f in range(8):
            for h in range(2):
                at = j * 64 + h * 32
                rows[at : at + 32, f * 128 : f * 128 + 128] = r4[j, 2 * f + h]

    def fifth(k):
        device, place = row_peer(k)
        return remote(gu.at[place], r5.at[y], ss5.at[k], rs5.at[k], device)

    def project(place):
        block = rows[pl.ds(pl.multiple_of(place * 128, 128), 128), :]
        gu[place] = jnp.dot(block, w_ref[...], preferred_element_type=F32)

    @pl.loop(1, NY)
    def _(k):
        _, place = row_peer(k)
        project(place)
        fifth(k).start()

    project(y)
    r5[y] = gu[y]

    @pl.loop(1, NO)
    def _(k):
        for each in copies(k):
            each.wait()

    @pl.loop(1, NY)
    def _(k):
        fifth(k).wait()

    for k in range(1, NX):
        along_x(k).wait_send()
    for k in range(NX):
        across(k).wait_send()

    both = (r5[0] + r5[1]) + (r5[2] + r5[3])
    gate, up = both[:, :128], both[:, 128:]
    mixed = gate / (1.0 + jnp.exp(-gate)) * up
    score_ref[...] = lax.dot_general(
        ws_ref[...],
        mixed,
        (((1,), (1,)), ((), ())),
        precision=lax.Precision.HIGHEST,
        preferred_element_type=F32,
    )


def exchange(rows, slots, r3, w, ws):
    ns = NX * NC
    dma = pltpu.SemaphoreType.DMA
    return pl.pallas_call(
        exchange_kernel,
        out_shape=(
            jax.ShapeDtypeStruct(rows.shape, rows.dtype),
            jax.ShapeDtypeStruct(slots.shape, slots.dtype),
            jax.ShapeDtypeStruct((8, 128), F32),
        ),
        in_specs=[VM] * 5,
        out_specs=(VM, VM, VM),
        scratch_shapes=[
            pltpu.VMEM((ns, NZ, 32, 128), BF),
            pltpu.VMEM((512, 1024), BF),
            pltpu.VMEM((NY, 128, 256), F32),
            pltpu.VMEM((NY, 128, 256), F32),
            dma((NO,)), dma((NO,)), dma((NO,)), dma((NO,)),
            dma((NX,)), dma((NX,)), dma((NX,)), dma((NX,)), dma((NY,)), dma((NY,)),
        ],
        compiler_params=pltpu.CompilerParams(collective_id=1, has_side_effects=True),
    )(rows, slots, r3, w, ws)


def return_kernel(
    ret_ref, score_ref, table_ref, out_ref, r1, s2, c1, d2, c2,
    ss1, rs1, cs1, cr1, ss2, rs2, cs2, cr2,
):
    ns = NX * NC
    _, me = plane_peer(0)
    _, side = side_peer(0)
    _, z, _, _ = here()
    greet(plane_peer, NO)
    greet(line_peer, NZ)
    pl.semaphore_wait(pltpu.get_barrier_semaphore(), NO + NZ - 2)

    def back(k):
        device, place = plane_peer(k)
        return remote(ret_ref.at[place], r1.at[me], ss1.at[k], rs1.at[k], device)

    def score1(k):
        device, _ = side_peer(k)
        return remote(score_ref, c1.at[side], cs1.at[k], cr1.at[k], device)

    @pl.loop(1, NO)
    def _(k):
        back(k).start()

    @pl.loop(1, ns)
    def _(k):
        score1(k).start()

    r1[me] = ret_ref[me]
    c1[side] = score_ref[...]

    @pl.loop(1, NO)
    def _(k):
        back(k).wait()

    @pl.loop(1, ns)
    def _(k):
        score1(k).wait()

    total = r1[0]
    for j in range(1, NO):
        total = total + r1[j]
    s2[...] = total
    total = c1[0]
    for j in range(1, ns):
        total = total + c1[j]
    d2[...] = total

    def line(k):
        device, place = line_peer(k)
        return (
            remote(s2.at[place], table_ref.at[z], ss2.at[k], rs2.at[k], device),
            remote(d2, c2.at[z], cs2.at[k], cr2.at[k], device),
        )

    @pl.loop(1, NZ)
    def _(k):
        for each in line(k):
            each.start()

    table_ref[z] = s2[z]
    c2[z] = d2[...]

    @pl.loop(1, NZ)
    def _(k):
        for each in line(k):
            each.wait()

    total = c2[0]
    for j in range(1, NZ):
        total = total + c2[j]
    out_ref[...] = total[:1]


def give_back(ret, score):
    ns = NX * NC
    dma = pltpu.SemaphoreType.DMA
    return pl.pallas_call(
        return_kernel,
        out_shape=(
            jax.ShapeDtypeStruct((NZ, 1, 128), F32),
            jax.ShapeDtypeStruct((1, 128), F32),
        ),
        in_specs=[VM, VM],
        out_specs=(VM, VM),
        scratch_shapes=[
            pltpu.VMEM((NO, NZ, 1, 128), F32),
            pltpu.VMEM((NZ, 1, 128), F32),
            pltpu.VMEM((ns, 8, 128), F32),
            pltpu.VMEM((8, 128), F32),
            pltpu.VMEM((NZ, 8, 128), F32),
            dma((NO,)), dma((NO,)), dma((ns,)), dma((ns,)),
            dma((NZ,)), dma((NZ,)), dma((NZ,)), dma((NZ,)),
        ],
        compiler_params=pltpu.CompilerParams(collective_id=3, has_side_effects=True),
    )(ret, score)


def body(
    queries,
    class_in,
    class_out,
    passages,
    bucket_sizes,
    bucket_owner,
    bucket_slot,
    embed,
    w_gate,
    w_up,
    w_score,
    block_tokens,
):
    x, z, c, y = here()
    mine = (x * NC + c) * NY + y
    rows, top = bucket_owner.shape
    width = queries.shape[1]
    i32 = jnp.int32

    owner_flat = bucket_owner.reshape(rows * top)
    order = jnp.arange(rows * top, dtype=i32)
    earlier = (owner_flat[:, None] == owner_flat[None, :]) & (order[None, :] < order[:, None])
    rank = jnp.sum(earlier.astype(i32), axis=1).reshape(rows, top)
    own_y = bucket_owner % NY
    own_c = (bucket_owner // NY) % NC
    own_z = (bucket_owner // (NY * NC)) % NZ
    own_x = bucket_owner // (NY * NC * NZ)
    own_o = (own_x * NC + own_c) * NY + own_y
    code = (own_z * NO + own_o) * 2 + rank
    ints = jnp.concatenate([code.T, bucket_slot.T + 1], axis=0)
    ints = jnp.pad(ints, ((0, 0), (0, 128 - rows)))

    vocab_rows = embed.shape[0]
    local_ids = block_tokens.reshape(-1) - ((x * NZ + z) * NC + c) * vocab_rows
    picks = (local_ids[:, None] == jnp.arange(vocab_rows, dtype=i32)[None, :]).astype(BF)
    fill = 128 - w_gate.shape[1]
    w = jnp.concatenate(
        [jnp.pad(w_gate, ((0, 0), (0, fill))), jnp.pad(w_up, ((0, 0), (0, fill)))], axis=1
    )
    ws = jnp.broadcast_to(jnp.pad(w_score.astype(F32), (0, fill))[None, :], (8, 128))
    line_rows, line_ints, line_tokens = gather_line(
        queries.reshape(2, rows // 2, width), ints, picks.reshape(NX * NC, 64, vocab_rows), embed
    )
    line_rows = line_rows.reshape(NZ * rows, width)
    line_code = line_ints[:, :top, :rows].transpose(1, 0, 2).reshape(top, NZ * rows)
    line_slot = line_ints[:, top : 2 * top, :rows].transpose(1, 0, 2).reshape(top, NZ * rows)
    wanted = z * NO + jnp.arange(NO, dtype=i32)
    hit = (line_code // 2)[None, :, :] == wanted[:, None, None]
    turn = jnp.sum(jnp.where(hit, line_code[None] % 2 + 1, 0), axis=1)
    slot_of = jnp.sum(jnp.where(hit, line_slot[None], 0), axis=1)
    place = jnp.arange(NZ * 2, dtype=i32)
    col = jnp.arange(NZ * rows, dtype=i32)
    chosen = (turn[:, None, :] == (place % 2 + 1)[None, :, None]) & (
        (place // 2)[:, None] == (col // rows)[None, :]
    )[None]
    send_slots = jnp.sum(jnp.where(chosen, slot_of[:, None, :], 0), axis=2)
    send_rows = jnp.dot(
        chosen.astype(BF).reshape(NO * NZ * 2, NZ * rows), line_rows, preferred_element_type=F32
    ).astype(BF)
    send_slots = jnp.pad(send_slots, ((0, 0), (0, 128 - 2 * NZ))).reshape(NO, 1, 128)
    got_rows, got_slots, score = exchange(
        send_rows.reshape(NO, NZ * 2, width), send_slots, line_tokens, w, ws
    )
    got_rows = got_rows.reshape(NO * NZ * 2, width)
    got_slots = got_slots.reshape(NO, 128)[:, : 2 * NZ].reshape(NO * NZ * 2) - 1

    hidden = jax.nn.relu(jnp.dot(got_rows, class_in, preferred_element_type=F32)).astype(BF)
    all_logits = jnp.dot(hidden, class_out, preferred_element_type=F32)
    columns = jnp.arange(class_out.shape[1], dtype=i32)
    slot_logit = jnp.sum(jnp.where(got_slots[:, None] == columns[None, :], all_logits, 0.0), axis=1)
    bucket_end = jnp.cumsum(bucket_sizes.reshape(-1))
    positions = jnp.arange(passages.shape[0], dtype=i32)
    passage_bucket = jnp.sum((bucket_end[:, None] <= positions[None, :]).astype(i32), axis=0)
    similar = jnp.einsum("sd,pd->sp", got_rows, passages, preferred_element_type=F32)
    slot_mass = jnp.sum(
        jnp.where(got_slots[:, None] == passage_bucket[None, :], jnp.exp(similar), 0.0), axis=1
    )
    lane = jnp.arange(128, dtype=i32)
    logit3 = slot_logit.reshape(NO, NZ, 2)
    mass3 = slot_mass.reshape(NO, NZ, 2)
    odd = lane % 2 == 1
    spread = jnp.where(
        lane < 64,
        jnp.where(odd, logit3[:, :, 1:], logit3[:, :, :1]),
        jnp.where(odd, mass3[:, :, 1:], mass3[:, :, :1]),
    )
    ret = jnp.where((lane % 64) // 2 == mine, spread, 0.0).reshape(NO, NZ, 1, 128)

    table, token_scores = give_back(ret, score)
    table = table.reshape(NZ, 128)
    logit_table = table[:, :64].reshape(NZ * 64)
    mass_table = table[:, 64:].reshape(NZ * 64)
    pick = code.reshape(-1)[:, None] == jnp.arange(NZ * 64, dtype=i32)[None, :]
    bucket_logit = jnp.sum(jnp.where(pick, logit_table[None], 0.0), axis=1).reshape(rows, top)
    bucket_mass = jnp.sum(jnp.where(pick, mass_table[None], 0.0), axis=1).reshape(rows, top)
    return (bucket_logit, bucket_mass, token_scores)


def solution(mesh):
    fine = Mesh(mesh.devices.reshape(NX, NZ, NC, NY), AXES)
    group = ("x", "z", "c")
    placed = (
        P(AXES, None),
        P(),
        P(None, AXES),
        P(AXES, None),
        P(AXES, None),
        P(AXES, None),
        P(AXES, None),
        P(group, "y"),
        P("y", group),
        P("y", group),
        P(group),
        P(),
    )
    return jax.shard_map(
        body,
        mesh=fine,
        in_specs=placed,
        out_specs=(P(AXES, None), P(AXES, None), P("y", None)),
        check_vma=False,
    )
```

```python
import jax
import jax.numpy as jnp
from jax import lax
from jax.experimental import pallas as pl
from jax.experimental.pallas import tpu as pltpu
from jax.sharding import Mesh, PartitionSpec as P

AXES = ("x", "z", "c", "y")
NX, NZ, NC, NY = 4, 16, 2, 4
NO = NX * NC * NY
BF = jnp.bfloat16
F32 = jnp.float32
SECOND, THIRD = 3, 6
VM = pl.BlockSpec(memory_space=pltpu.VMEM)


def here():
    return tuple(lax.axis_index(a) for a in AXES)


def remote(src, dst, send, recv, device):
    return pltpu.make_async_remote_copy(
        src_ref=src,
        dst_ref=dst,
        send_sem=send,
        recv_sem=recv,
        device_id=device,
        device_id_type=pl.DeviceIdType.MESH,
    )


def greet(peers_of, count):
    barrier = pltpu.get_barrier_semaphore()

    @pl.loop(1, count)
    def _(k):
        device, _ = peers_of(k)
        pl.semaphore_signal(barrier, inc=1, device_id=device, device_id_type=pl.DeviceIdType.MESH)


def plane_peer(k):
    x, z, c, y = here()
    px = lax.rem(x + k // (NC * NY), NX)
    pc = lax.rem(c + lax.rem(k // NY, NC), NC)
    py = lax.rem(y + lax.rem(k, NY), NY)
    return (px, z, pc, py), (px * NC + pc) * NY + py


def side_peer(k):
    x, z, c, y = here()
    px = lax.rem(x + k // NC, NX)
    pc = lax.rem(c + lax.rem(k, NC), NC)
    return (px, z, pc, y), px * NC + pc


def line_peer(k):
    x, z, c, y = here()
    pz = lax.rem(z + k, NZ)
    return (x, pz, c, y), pz


def row_peer(k):
    x, z, c, y = here()
    py = lax.rem(y + k, NY)
    return (x, z, c, py), py


def line_kernel(
    q_ref, i_ref, picks_ref, embed_ref, out_ref, iout_ref, r3_ref,
    p1, pc, q1, r1, s2, r2, s3, send_sem, recv_sem, sc, rc, ss1, rs1, ss2, rs2, ss3, rs3,
):
    ns = NX * NC
    x, z, c, y = here()
    _, me = side_peer(0)
    right = (x, lax.rem(z + 1, NZ), c, y)
    left = (x, lax.rem(z + NZ - 1, NZ), c, y)
    greet(line_peer, NZ)
    greet(side_peer, ns)
    pl.semaphore_wait(pltpu.get_barrier_semaphore(), NZ + ns - 2)
    partner = (x, z, 1 - c, y)

    def copy(way, step, part):
        place = lax.rem(z + (NZ - step if way == 0 else step), NZ)
        device = right if way == 0 else left
        if part < 2:
            src = q_ref.at[part] if step == 0 else out_ref.at[place, part]
            dst = out_ref.at[place, part]
        else:
            src = i_ref if step == 0 else iout_ref.at[place]
            dst = iout_ref.at[place]
        return remote(src, dst, send_sem.at[way, step, part], recv_sem.at[way, step, part], device)

    def partial(place):
        part = jnp.dot(picks_ref[place], embed_ref[...], preferred_element_type=F32).astype(BF)
        for f in range(8):
            for h in range(2):
                p1[place, 2 * f + h] = part[h * 32 : h * 32 + 32, f * 128 : f * 128 + 128]

    def swap(px):
        return remote(p1.at[px * NC + 1 - c], pc.at[px], sc.at[px], rc.at[px], partner)

    def first(k):
        px = lax.rem(x + k, NX)
        return remote(q1.at[px], r1.at[x], ss1.at[k], rs1.at[k], (px, z, c, y))

    def second(k):
        device, place = line_peer(k)
        return remote(s2.at[place], r2.at[z], ss2.at[k], rs2.at[k], device)

    def third(k):
        device, _ = line_peer(k)
        return remote(s3, r3_ref.at[z], ss3.at[k], rs3.at[k], device)

    def start_second():
        for k in range(1, NX):
            first(k).wait()
        s2[...] = (r1[0] + r1[1]) + (r1[2] + r1[3])

        @pl.loop(1, NZ)
        def _(k):
            second(k).start()

        r2[z] = s2[z]

    def start_third():
        @pl.loop(1, NZ)
        def _(k):
            second(k).wait()

        total = r2[0]
        for j in range(1, NZ):
            total = total + r2[j]
        s3[...] = total

        @pl.loop(1, NZ)
        def _(k):
            third(k).start()

        r3_ref[z] = s3[...]

    started = {}
    for step in range(NZ // 2):
        for part in (2, 0, 1):
            for way in (0, 1):
                if step > 0 and (way, step - 1, part) in started:
                    started[way, step - 1, part].wait_recv()
                if way == 1 and step == NZ // 2 - 1:
                    continue
                started[way, step, part] = copy(way, step, part)
                started[way, step, part].start()
        if step == 0:

            @pl.loop(0, NX)
            def _(px):
                partial(px * NC + 1 - c)
                swap(px).start()

            @pl.loop(0, NX)
            def _(px):
                partial(px * NC + c)

        if step == 1:
            for k in (2, 1, 3, 0):
                px = lax.rem(x + k, NX)
                swap(px).wait()
                q1[px] = p1[px * NC + c] + pc[px]
                if k:
                    first(k).start()
            r1[x] = q1[x]
            out_ref[z] = q_ref[...]
            iout_ref[z] = i_ref[...]
        if step == SECOND:
            start_second()
        if step == THIRD:
            start_third()
    for (way, step, part), done in started.items():
        if way == 0 and step == NZ // 2 - 1:
            done.wait_recv()
        done.wait_send()

    @pl.loop(1, NZ)
    def _(k):
        third(k).wait()


def gather_line(rows, ints, picks, embed):
    ns = NX * NC
    dma = pltpu.SemaphoreType.DMA
    return pl.pallas_call(
        line_kernel,
        out_shape=(
            jax.ShapeDtypeStruct((NZ,) + rows.shape, rows.dtype),
            jax.ShapeDtypeStruct((NZ,) + ints.shape, ints.dtype),
            jax.ShapeDtypeStruct((NZ, 32, 128), BF),
        ),
        in_specs=[VM] * 4,
        out_specs=(VM, VM, VM),
        scratch_shapes=[
            pltpu.VMEM((ns, NZ, 32, 128), BF),
            pltpu.VMEM((NX, NZ, 32, 128), BF),
            pltpu.VMEM((NX, NZ, 32, 128), BF),
            pltpu.VMEM((NX, NZ, 32, 128), BF),
            pltpu.VMEM((NZ, 32, 128), BF),
            pltpu.VMEM((NZ, 32, 128), BF),
            pltpu.VMEM((32, 128), BF),
            dma((2, NZ // 2, 3)), dma((2, NZ // 2, 3)), dma((NX,)), dma((NX,)),
            dma((NX,)), dma((NX,)), dma((NZ,)), dma((NZ,)), dma((NZ,)), dma((NZ,)),
        ],
        compiler_params=pltpu.CompilerParams(collective_id=0, has_side_effects=True),
    )(rows, ints, picks, embed)


def exchange_kernel(
    q_ref, s_ref, r3_ref, w_ref, ws_ref, out_ref, sout_ref, score_ref,
    r4, rows, gu, r5, send_sem, recv_sem, ssend, srecv, ss4, rs4, sc4, rc4, ss5, rs5,
):
    x, z, c, y = here()
    ns = NX * NC
    _, me = plane_peer(0)
    greet(plane_peer, NO)
    pl.semaphore_wait(pltpu.get_barrier_semaphore(), NO - 1)
    partner = (x, z, 1 - c, y)

    def along_x(k):
        device = (lax.rem(x + k, NX), z, c, y)
        return remote(r3_ref, r4.at[x * NC + c], ss4.at[k], rs4.at[k], device)

    def across(k):
        place = lax.rem(x + NX - k, NX) * NC + c
        return remote(r4.at[place], r4.at[place], sc4.at[k], rc4.at[k], partner)

    def copies(k):
        device, place = plane_peer(k)
        return (
            remote(q_ref.at[place], out_ref.at[me], send_sem.at[k], recv_sem.at[k], device),
            remote(s_ref.at[place], sout_ref.at[me], ssend.at[k], srecv.at[k], device),
        )

    for k in (2, 1, 3):
        along_x(k).start()
    r4[x * NC + c] = r3_ref[...]
    across(0).start()

    @pl.loop(1, NO)
    def _(k):
        for each in copies(k):
            each.start()

    out_ref[me] = q_ref[me]
    sout_ref[me] = s_ref[me]

    for k in (1, 3, 2):
        along_x(k).wait_recv()
        across(k).start()
    for k in range(NX):
        across(k).wait_recv()

    for j in range(ns):
        for f in range(8):
            for h in range(2):
                at = j * 64 + h * 32
                rows[at : at + 32, f * 128 : f * 128 + 128] = r4[j, 2 * f + h]

    def fifth(k):
        device, place = row_peer(k)
        return remote(gu.at[place], r5.at[y], ss5.at[k], rs5.at[k], device)

    def project(place):
        block = rows[pl.ds(pl.multiple_of(place * 128, 128), 128), :]
        gu[place] = jnp.dot(block, w_ref[...], preferred_element_type=F32)

    @pl.loop(1, NY)
    def _(k):
        _, place = row_peer(k)
        project(place)
        fifth(k).start()

    project(y)
    r5[y] = gu[y]

    @pl.loop(1, NO)
    def _(k):
        for each in copies(k):
            each.wait()

    @pl.loop(1, NY)
    def _(k):
        fifth(k).wait()

    for k in range(1, NX):
        along_x(k).wait_send()
    for k in range(NX):
        across(k).wait_send()

    both = (r5[0] + r5[1]) + (r5[2] + r5[3])
    gate, up = both[:, :128], both[:, 128:]
    mixed = gate / (1.0 + jnp.exp(-gate)) * up
    score_ref[...] = lax.dot_general(
        ws_ref[...],
        mixed,
        (((1,), (1,)), ((), ())),
        precision=lax.Precision.HIGHEST,
        preferred_element_type=F32,
    )


def exchange(rows, slots, r3, w, ws):
    ns = NX * NC
    dma = pltpu.SemaphoreType.DMA
    return pl.pallas_call(
        exchange_kernel,
        out_shape=(
            jax.ShapeDtypeStruct(rows.shape, rows.dtype),
            jax.ShapeDtypeStruct(slots.shape, slots.dtype),
            jax.ShapeDtypeStruct((8, 128), F32),
        ),
        in_specs=[VM] * 5,
        out_specs=(VM, VM, VM),
        scratch_shapes=[
            pltpu.VMEM((ns, NZ, 32, 128), BF),
            pltpu.VMEM((512, 1024), BF),
            pltpu.VMEM((NY, 128, 256), F32),
            pltpu.VMEM((NY, 128, 256), F32),
            dma((NO,)), dma((NO,)), dma((NO,)), dma((NO,)),
            dma((NX,)), dma((NX,)), dma((NX,)), dma((NX,)), dma((NY,)), dma((NY,)),
        ],
        compiler_params=pltpu.CompilerParams(collective_id=1, has_side_effects=True),
    )(rows, slots, r3, w, ws)


def return_kernel(
    ret_ref, score_ref, table_ref, out_ref, r1, s2, c1, d2, c2,
    ss1, rs1, cs1, cr1, ss2, rs2, cs2, cr2,
):
    ns = NX * NC
    _, me = plane_peer(0)
    _, side = side_peer(0)
    _, z, _, _ = here()
    greet(plane_peer, NO)
    greet(line_peer, NZ)
    pl.semaphore_wait(pltpu.get_barrier_semaphore(), NO + NZ - 2)

    def back(k):
        device, place = plane_peer(k)
        return remote(ret_ref.at[place], r1.at[me], ss1.at[k], rs1.at[k], device)

    def score1(k):
        device, _ = side_peer(k)
        return remote(score_ref, c1.at[side], cs1.at[k], cr1.at[k], device)

    @pl.loop(1, NO)
    def _(k):
        back(k).start()

    @pl.loop(1, ns)
    def _(k):
        score1(k).start()

    r1[me] = ret_ref[me]
    c1[side] = score_ref[...]

    @pl.loop(1, NO)
    def _(k):
        back(k).wait()

    @pl.loop(1, ns)
    def _(k):
        score1(k).wait()

    total = r1[0]
    for j in range(1, NO):
        total = total + r1[j]
    for i in range(NZ):
        s2[i] = total[i : i + 1]
    total = c1[0]
    for j in range(1, ns):
        total = total + c1[j]
    d2[...] = total

    def line(k):
        device, place = line_peer(k)
        return (
            remote(s2.at[place], table_ref.at[z], ss2.at[k], rs2.at[k], device),
            remote(d2, c2.at[z], cs2.at[k], cr2.at[k], device),
        )

    @pl.loop(1, NZ)
    def _(k):
        for each in line(k):
            each.start()

    table_ref[z] = s2[z]
    c2[z] = d2[...]

    @pl.loop(1, NZ)
    def _(k):
        for each in line(k):
            each.wait()

    total = c2[0]
    for j in range(1, NZ):
        total = total + c2[j]
    out_ref[...] = total[:1]


def give_back(ret, score):
    ns = NX * NC
    dma = pltpu.SemaphoreType.DMA
    return pl.pallas_call(
        return_kernel,
        out_shape=(
            jax.ShapeDtypeStruct((NZ, 1, 128), F32),
            jax.ShapeDtypeStruct((1, 128), F32),
        ),
        in_specs=[VM, VM],
        out_specs=(VM, VM),
        scratch_shapes=[
            pltpu.VMEM((NO, NZ, 128), F32),
            pltpu.VMEM((NZ, 1, 128), F32),
            pltpu.VMEM((ns, 8, 128), F32),
            pltpu.VMEM((8, 128), F32),
            pltpu.VMEM((NZ, 8, 128), F32),
            dma((NO,)), dma((NO,)), dma((ns,)), dma((ns,)),
            dma((NZ,)), dma((NZ,)), dma((NZ,)), dma((NZ,)),
        ],
        compiler_params=pltpu.CompilerParams(collective_id=3, has_side_effects=True),
    )(ret, score)


def body(
    queries,
    class_in,
    class_out,
    passages,
    bucket_sizes,
    bucket_owner,
    bucket_slot,
    embed,
    w_gate,
    w_up,
    w_score,
    block_tokens,
):
    x, z, c, y = here()
    mine = (x * NC + c) * NY + y
    rows, top = bucket_owner.shape
    width = queries.shape[1]
    i32 = jnp.int32

    owner_flat = bucket_owner.reshape(rows * top)
    order = jnp.arange(rows * top, dtype=i32)
    earlier = (owner_flat[:, None] == owner_flat[None, :]) & (order[None, :] < order[:, None])
    rank = jnp.sum(earlier.astype(i32), axis=1).reshape(rows, top)
    own_y = bucket_owner % NY
    own_c = (bucket_owner // NY) % NC
    own_z = (bucket_owner // (NY * NC)) % NZ
    own_x = bucket_owner // (NY * NC * NZ)
    own_o = (own_x * NC + own_c) * NY + own_y
    code = (own_z * NO + own_o) * 2 + rank
    ints = jnp.concatenate([code.T, bucket_slot.T + 1], axis=0)
    ints = jnp.pad(ints, ((0, 0), (0, 128 - rows)))

    vocab_rows = embed.shape[0]
    local_ids = block_tokens.reshape(-1) - ((x * NZ + z) * NC + c) * vocab_rows
    picks = (local_ids[:, None] == jnp.arange(vocab_rows, dtype=i32)[None, :]).astype(BF)
    fill = 128 - w_gate.shape[1]
    w = jnp.concatenate(
        [jnp.pad(w_gate, ((0, 0), (0, fill))), jnp.pad(w_up, ((0, 0), (0, fill)))], axis=1
    )
    ws = jnp.broadcast_to(jnp.pad(w_score.astype(F32), (0, fill))[None, :], (8, 128))
    line_rows, line_ints, line_tokens = gather_line(
        queries.reshape(2, rows // 2, width), ints, picks.reshape(NX * NC, 64, vocab_rows), embed
    )
    line_rows = line_rows.reshape(NZ * rows, width)
    line_code = line_ints[:, :top, :rows].transpose(1, 0, 2).reshape(top, NZ * rows)
    line_slot = line_ints[:, top : 2 * top, :rows].transpose(1, 0, 2).reshape(top, NZ * rows)
    wanted = z * NO + jnp.arange(NO, dtype=i32)
    hit = (line_code // 2)[None, :, :] == wanted[:, None, None]
    turn = jnp.sum(jnp.where(hit, line_code[None] % 2 + 1, 0), axis=1)
    slot_of = jnp.sum(jnp.where(hit, line_slot[None], 0), axis=1)
    place = jnp.arange(NZ * 2, dtype=i32)
    col = jnp.arange(NZ * rows, dtype=i32)
    chosen = (turn[:, None, :] == (place % 2 + 1)[None, :, None]) & (
        (place // 2)[:, None] == (col // rows)[None, :]
    )[None]
    send_slots = jnp.sum(jnp.where(chosen, slot_of[:, None, :], 0), axis=2)
    send_rows = jnp.dot(
        chosen.astype(BF).reshape(NO * NZ * 2, NZ * rows), line_rows, preferred_element_type=F32
    ).astype(BF)
    send_slots = jnp.pad(send_slots, ((0, 0), (0, 128 - 2 * NZ))).reshape(NO, 1, 128)
    got_rows, got_slots, score = exchange(
        send_rows.reshape(NO, NZ * 2, width), send_slots, line_tokens, w, ws
    )
    got_rows = got_rows.reshape(NO * NZ * 2, width)
    got_slots = got_slots.reshape(NO, 128)[:, : 2 * NZ].reshape(NO * NZ * 2) - 1

    hidden = jax.nn.relu(jnp.dot(got_rows, class_in, preferred_element_type=F32)).astype(BF)
    all_logits = jnp.dot(hidden, class_out, preferred_element_type=F32)
    columns = jnp.arange(class_out.shape[1], dtype=i32)
    slot_logit = jnp.sum(jnp.where(got_slots[:, None] == columns[None, :], all_logits, 0.0), axis=1)
    bucket_end = jnp.cumsum(bucket_sizes.reshape(-1))
    positions = jnp.arange(passages.shape[0], dtype=i32)
    passage_bucket = jnp.sum((bucket_end[:, None] <= positions[None, :]).astype(i32), axis=0)
    similar = jnp.einsum("sd,pd->sp", got_rows, passages, preferred_element_type=F32)
    slot_mass = jnp.sum(
        jnp.where(got_slots[:, None] == passage_bucket[None, :], jnp.exp(similar), 0.0), axis=1
    )
    lane = jnp.arange(128, dtype=i32)
    logit3 = slot_logit.reshape(NO, NZ, 2)
    mass3 = slot_mass.reshape(NO, NZ, 2)
    odd = lane % 2 == 1
    spread = jnp.where(
        lane < 64,
        jnp.where(odd, logit3[:, :, 1:], logit3[:, :, :1]),
        jnp.where(odd, mass3[:, :, 1:], mass3[:, :, :1]),
    )
    ret = jnp.where((lane % 64) // 2 == mine, spread, 0.0)

    table, token_scores = give_back(ret, score)
    table = table.reshape(NZ, 128)
    logit_table = table[:, :64].reshape(NZ * 64)
    mass_table = table[:, 64:].reshape(NZ * 64)
    pick = code.reshape(-1)[:, None] == jnp.arange(NZ * 64, dtype=i32)[None, :]
    bucket_logit = jnp.sum(jnp.where(pick, logit_table[None], 0.0), axis=1).reshape(rows, top)
    bucket_mass = jnp.sum(jnp.where(pick, mass_table[None], 0.0), axis=1).reshape(rows, top)
    return (bucket_logit, bucket_mass, token_scores)


def solution(mesh):
    fine = Mesh(mesh.devices.reshape(NX, NZ, NC, NY), AXES)
    group = ("x", "z", "c")
    placed = (
        P(AXES, None),
        P(),
        P(None, AXES),
        P(AXES, None),
        P(AXES, None),
        P(AXES, None),
        P(AXES, None),
        P(group, "y"),
        P("y", group),
        P("y", group),
        P(group),
        P(),
    )
    return jax.shard_map(
        body,
        mesh=fine,
        in_specs=placed,
        out_specs=(P(AXES, None), P(AXES, None), P("y", None)),
        check_vma=False,
    )
```

```python
import jax
import jax.numpy as jnp
from jax import lax
from jax.experimental import pallas as pl
from jax.experimental.pallas import tpu as pltpu
from jax.sharding import Mesh, PartitionSpec as P

AXES = ("x", "z", "c", "y")
NX, NZ, NC, NY = 4, 16, 2, 4
NO = NX * NC * NY
BF = jnp.bfloat16
F32 = jnp.float32
STRIDE = 11
SECOND, THIRD = 3, 6
VM = pl.BlockSpec(memory_space=pltpu.VMEM)


def here():
    return tuple(lax.axis_index(a) for a in AXES)


def remote(src, dst, send, recv, device):
    return pltpu.make_async_remote_copy(
        src_ref=src,
        dst_ref=dst,
        send_sem=send,
        recv_sem=recv,
        device_id=device,
        device_id_type=pl.DeviceIdType.MESH,
    )


def greet(peers_of, count):
    barrier = pltpu.get_barrier_semaphore()

    @pl.loop(1, count)
    def _(k):
        device, _ = peers_of(k)
        pl.semaphore_signal(barrier, inc=1, device_id=device, device_id_type=pl.DeviceIdType.MESH)


def plane_peer(k):
    x, z, c, y = here()
    px = lax.rem(x + k // (NC * NY), NX)
    pc = lax.rem(c + lax.rem(k // NY, NC), NC)
    py = lax.rem(y + lax.rem(k, NY), NY)
    return (px, z, pc, py), (px * NC + pc) * NY + py


def side_peer(k):
    x, z, c, y = here()
    px = lax.rem(x + k // NC, NX)
    pc = lax.rem(c + lax.rem(k, NC), NC)
    return (px, z, pc, y), px * NC + pc


def line_peer(k):
    x, z, c, y = here()
    pz = lax.rem(z + k, NZ)
    return (x, pz, c, y), pz


def row_peer(k):
    x, z, c, y = here()
    py = lax.rem(y + k, NY)
    return (x, z, c, py), py


def line_kernel(
    q_ref, i_ref, picks_ref, embed_ref, out_ref, iout_ref, r3_ref,
    p1, pc, q1, r1, s2, r2, s3, send_sem, recv_sem, sc, rc, ss1, rs1, ss2, rs2, ss3, rs3,
):
    ns = NX * NC
    x, z, c, y = here()
    _, me = side_peer(0)
    right = (x, lax.rem(z + 1, NZ), c, y)
    left = (x, lax.rem(z + NZ - 1, NZ), c, y)
    greet(line_peer, NZ)
    greet(side_peer, ns)
    pl.semaphore_wait(pltpu.get_barrier_semaphore(), NZ + ns - 2)
    partner = (x, z, 1 - c, y)

    def copy(way, step, part):
        place = lax.rem(z + (NZ - step if way == 0 else step), NZ)
        device = right if way == 0 else left
        if part < 2:
            src = q_ref.at[part] if step == 0 else out_ref.at[place, part]
            dst = out_ref.at[place, part]
        else:
            src = i_ref if step == 0 else iout_ref.at[place]
            dst = iout_ref.at[place]
        return remote(src, dst, send_sem.at[way, step, part], recv_sem.at[way, step, part], device)

    def partial(place):
        part = jnp.dot(picks_ref[place], embed_ref[...], preferred_element_type=F32).astype(BF)
        for f in range(8):
            for h in range(2):
                p1[place, 2 * f + h] = part[h * 32 : h * 32 + 32, f * 128 : f * 128 + 128]

    def swap(px):
        return remote(p1.at[px * NC + 1 - c], pc.at[px], sc.at[px], rc.at[px], partner)

    def first(k):
        px = lax.rem(x + k, NX)
        return remote(q1.at[px], r1.at[x], ss1.at[k], rs1.at[k], (px, z, c, y))

    def second(k):
        device, place = line_peer(k)
        return remote(s2.at[place], r2.at[z], ss2.at[k], rs2.at[k], device)

    def third(k):
        device, _ = line_peer(k)
        return remote(s3, r3_ref.at[z], ss3.at[k], rs3.at[k], device)

    def start_second():
        for k in range(1, NX):
            first(k).wait()
        s2[...] = (r1[0] + r1[1]) + (r1[2] + r1[3])

        @pl.loop(1, NZ)
        def _(k):
            second(k).start()

        r2[z] = s2[z]

    def start_third():
        @pl.loop(1, NZ)
        def _(k):
            second(k).wait()

        total = r2[0]
        for j in range(1, NZ):
            total = total + r2[j]
        s3[...] = total

        @pl.loop(1, NZ)
        def _(k):
            third(k).start()

        r3_ref[z] = s3[...]

    started = {}
    for step in range(NZ // 2):
        for part in (2, 0, 1):
            for way in (0, 1):
                if step > 0 and (way, step - 1, part) in started:
                    started[way, step - 1, part].wait_recv()
                if way == 1 and step == NZ // 2 - 1:
                    continue
                started[way, step, part] = copy(way, step, part)
                started[way, step, part].start()
        if step == 0:

            @pl.loop(0, NX)
            def _(px):
                partial(px * NC + 1 - c)
                swap(px).start()

            @pl.loop(0, NX)
            def _(px):
                partial(px * NC + c)

        if step == 1:
            for k in (2, 1, 3, 0):
                px = lax.rem(x + k, NX)
                swap(px).wait()
                q1[px] = p1[px * NC + c] + pc[px]
                if k:
                    first(k).start()
            r1[x] = q1[x]
            out_ref[z] = q_ref[...]
            iout_ref[z] = i_ref[...]
        if step == SECOND:
            start_second()
        if step == THIRD:
            start_third()
    for (way, step, part), done in started.items():
        if way == 0 and step == NZ // 2 - 1:
            done.wait_recv()
        done.wait_send()

    @pl.loop(1, NZ)
    def _(k):
        third(k).wait()


def gather_line(rows, ints, picks, embed):
    ns = NX * NC
    dma = pltpu.SemaphoreType.DMA
    return pl.pallas_call(
        line_kernel,
        out_shape=(
            jax.ShapeDtypeStruct((NZ,) + rows.shape, rows.dtype),
            jax.ShapeDtypeStruct((NZ,) + ints.shape, ints.dtype),
            jax.ShapeDtypeStruct((NZ, 32, 128), BF),
        ),
        in_specs=[VM] * 4,
        out_specs=(VM, VM, VM),
        scratch_shapes=[
            pltpu.VMEM((ns, NZ, 32, 128), BF),
            pltpu.VMEM((NX, NZ, 32, 128), BF),
            pltpu.VMEM((NX, NZ, 32, 128), BF),
            pltpu.VMEM((NX, NZ, 32, 128), BF),
            pltpu.VMEM((NZ, 32, 128), BF),
            pltpu.VMEM((NZ, 32, 128), BF),
            pltpu.VMEM((32, 128), BF),
            dma((2, NZ // 2, 3)), dma((2, NZ // 2, 3)), dma((NX,)), dma((NX,)),
            dma((NX,)), dma((NX,)), dma((NZ,)), dma((NZ,)), dma((NZ,)), dma((NZ,)),
        ],
        compiler_params=pltpu.CompilerParams(collective_id=0, has_side_effects=True),
    )(rows, ints, picks, embed)


def exchange_kernel(
    q_ref, s_ref, r3_ref, w_ref, ws_ref, out_ref, sout_ref, score_ref,
    r4, rows, gu, r5, send_sem, recv_sem, ssend, srecv, ss4, rs4, sc4, rc4, ss5, rs5,
):
    x, z, c, y = here()
    ns = NX * NC
    _, me = plane_peer(0)
    greet(plane_peer, NO)
    pl.semaphore_wait(pltpu.get_barrier_semaphore(), NO - 1)
    partner = (x, z, 1 - c, y)

    def along_x(k):
        device = (lax.rem(x + k, NX), z, c, y)
        return remote(r3_ref, r4.at[x * NC + c], ss4.at[k], rs4.at[k], device)

    def across(k):
        place = lax.rem(x + NX - k, NX) * NC + c
        return remote(r4.at[place], r4.at[place], sc4.at[k], rc4.at[k], partner)

    def copies(k):
        device, place = plane_peer(k)
        return (
            remote(q_ref.at[place], out_ref.at[me], send_sem.at[k], recv_sem.at[k], device),
            remote(s_ref.at[place], sout_ref.at[me], ssend.at[k], srecv.at[k], device),
        )

    for k in (2, 1, 3):
        along_x(k).start()
    r4[x * NC + c] = r3_ref[...]
    across(0).start()

    @pl.loop(1, NO)
    def _(k):
        for each in copies(lax.rem(k * STRIDE, NO)):
            each.start()

    out_ref[me] = q_ref[me]
    sout_ref[me] = s_ref[me]

    for k in (1, 3, 2):
        along_x(k).wait_recv()
        across(k).start()
    for k in range(NX):
        across(k).wait_recv()

    for j in range(ns):
        for f in range(8):
            for h in range(2):
                at = j * 64 + h * 32
                rows[at : at + 32, f * 128 : f * 128 + 128] = r4[j, 2 * f + h]

    def fifth(k):
        device, place = row_peer(k)
        return remote(gu.at[place], r5.at[y], ss5.at[k], rs5.at[k], device)

    def project(place):
        block = rows[pl.ds(pl.multiple_of(place * 128, 128), 128), :]
        gu[place] = jnp.dot(block, w_ref[...], preferred_element_type=F32)

    @pl.loop(1, NY)
    def _(k):
        _, place = row_peer(k)
        project(place)
        fifth(k).start()

    project(y)
    r5[y] = gu[y]

    @pl.loop(1, NO)
    def _(k):
        for each in copies(k):
            each.wait()

    @pl.loop(1, NY)
    def _(k):
        fifth(k).wait()

    for k in range(1, NX):
        along_x(k).wait_send()
    for k in range(NX):
        across(k).wait_send()

    both = (r5[0] + r5[1]) + (r5[2] + r5[3])
    gate, up = both[:, :128], both[:, 128:]
    mixed = gate / (1.0 + jnp.exp(-gate)) * up
    score_ref[...] = lax.dot_general(
        ws_ref[...],
        mixed,
        (((1,), (1,)), ((), ())),
        precision=lax.Precision.HIGHEST,
        preferred_element_type=F32,
    )


def exchange(rows, slots, r3, w, ws):
    ns = NX * NC
    dma = pltpu.SemaphoreType.DMA
    return pl.pallas_call(
        exchange_kernel,
        out_shape=(
            jax.ShapeDtypeStruct(rows.shape, rows.dtype),
            jax.ShapeDtypeStruct(slots.shape, slots.dtype),
            jax.ShapeDtypeStruct((8, 128), F32),
        ),
        in_specs=[VM] * 5,
        out_specs=(VM, VM, VM),
        scratch_shapes=[
            pltpu.VMEM((ns, NZ, 32, 128), BF),
            pltpu.VMEM((512, 1024), BF),
            pltpu.VMEM((NY, 128, 256), F32),
            pltpu.VMEM((NY, 128, 256), F32),
            dma((NO,)), dma((NO,)), dma((NO,)), dma((NO,)),
            dma((NX,)), dma((NX,)), dma((NX,)), dma((NX,)), dma((NY,)), dma((NY,)),
        ],
        compiler_params=pltpu.CompilerParams(collective_id=1, has_side_effects=True),
    )(rows, slots, r3, w, ws)


def return_kernel(
    ret_ref, score_ref, table_ref, out_ref, r1, s2, c1, d2, c2,
    ss1, rs1, cs1, cr1, ss2, rs2, cs2, cr2,
):
    ns = NX * NC
    _, me = plane_peer(0)
    _, side = side_peer(0)
    _, z, _, _ = here()
    greet(plane_peer, NO)
    greet(line_peer, NZ)
    pl.semaphore_wait(pltpu.get_barrier_semaphore(), NO + NZ - 2)

    def back(k):
        device, place = plane_peer(k)
        return remote(ret_ref.at[place], r1.at[me], ss1.at[k], rs1.at[k], device)

    def score1(k):
        device, _ = side_peer(k)
        return remote(score_ref, c1.at[side], cs1.at[k], cr1.at[k], device)

    @pl.loop(1, NO)
    def _(k):
        back(k).start()

    @pl.loop(1, ns)
    def _(k):
        score1(k).start()

    r1[me] = ret_ref[me]
    c1[side] = score_ref[...]

    @pl.loop(1, NO)
    def _(k):
        back(k).wait()

    @pl.loop(1, ns)
    def _(k):
        score1(k).wait()

    total = r1[0]
    for j in range(1, NO):
        total = total + r1[j]
    for i in range(NZ):
        s2[i] = total[i : i + 1]
    total = c1[0]
    for j in range(1, ns):
        total = total + c1[j]
    d2[...] = total

    def line(k):
        device, place = line_peer(k)
        return (
            remote(s2.at[place], table_ref.at[z], ss2.at[k], rs2.at[k], device),
            remote(d2, c2.at[z], cs2.at[k], cr2.at[k], device),
        )

    @pl.loop(1, NZ)
    def _(k):
        for each in line(k):
            each.start()

    table_ref[z] = s2[z]
    c2[z] = d2[...]

    @pl.loop(1, NZ)
    def _(k):
        for each in line(k):
            each.wait()

    total = c2[0]
    for j in range(1, NZ):
        total = total + c2[j]
    out_ref[...] = total[:1]


def give_back(ret, score):
    ns = NX * NC
    dma = pltpu.SemaphoreType.DMA
    return pl.pallas_call(
        return_kernel,
        out_shape=(
            jax.ShapeDtypeStruct((NZ, 1, 128), F32),
            jax.ShapeDtypeStruct((1, 128), F32),
        ),
        in_specs=[VM, VM],
        out_specs=(VM, VM),
        scratch_shapes=[
            pltpu.VMEM((NO, NZ, 128), F32),
            pltpu.VMEM((NZ, 1, 128), F32),
            pltpu.VMEM((ns, 8, 128), F32),
            pltpu.VMEM((8, 128), F32),
            pltpu.VMEM((NZ, 8, 128), F32),
            dma((NO,)), dma((NO,)), dma((ns,)), dma((ns,)),
            dma((NZ,)), dma((NZ,)), dma((NZ,)), dma((NZ,)),
        ],
        compiler_params=pltpu.CompilerParams(collective_id=3, has_side_effects=True),
    )(ret, score)


def body(
    queries,
    class_in,
    class_out,
    passages,
    bucket_sizes,
    bucket_owner,
    bucket_slot,
    embed,
    w_gate,
    w_up,
    w_score,
    block_tokens,
):
    x, z, c, y = here()
    mine = (x * NC + c) * NY + y
    rows, top = bucket_owner.shape
    width = queries.shape[1]
    i32 = jnp.int32

    owner_flat = bucket_owner.reshape(rows * top)
    order = jnp.arange(rows * top, dtype=i32)
    earlier = (owner_flat[:, None] == owner_flat[None, :]) & (order[None, :] < order[:, None])
    rank = jnp.sum(earlier.astype(i32), axis=1).reshape(rows, top)
    own_y = bucket_owner % NY
    own_c = (bucket_owner // NY) % NC
    own_z = (bucket_owner // (NY * NC)) % NZ
    own_x = bucket_owner // (NY * NC * NZ)
    own_o = (own_x * NC + own_c) * NY + own_y
    code = (own_z * NO + own_o) * 2 + rank
    ints = jnp.concatenate([code.T, bucket_slot.T + 1], axis=0)
    ints = jnp.pad(ints, ((0, 0), (0, 128 - rows)))

    vocab_rows = embed.shape[0]
    local_ids = block_tokens.reshape(-1) - ((x * NZ + z) * NC + c) * vocab_rows
    picks = (local_ids[:, None] == jnp.arange(vocab_rows, dtype=i32)[None, :]).astype(BF)
    fill = 128 - w_gate.shape[1]
    w = jnp.concatenate(
        [jnp.pad(w_gate, ((0, 0), (0, fill))), jnp.pad(w_up, ((0, 0), (0, fill)))], axis=1
    )
    ws = jnp.broadcast_to(jnp.pad(w_score.astype(F32), (0, fill))[None, :], (8, 128))
    line_rows, line_ints, line_tokens = gather_line(
        queries.reshape(2, rows // 2, width), ints, picks.reshape(NX * NC, 64, vocab_rows), embed
    )
    line_rows = line_rows.reshape(NZ * rows, width)
    line_code = line_ints[:, :top, :rows].transpose(1, 0, 2).reshape(top, NZ * rows)
    line_slot = line_ints[:, top : 2 * top, :rows].transpose(1, 0, 2).reshape(top, NZ * rows)
    wanted = z * NO + jnp.arange(NO, dtype=i32)
    hit = (line_code // 2)[None, :, :] == wanted[:, None, None]
    turn = jnp.sum(jnp.where(hit, line_code[None] % 2 + 1, 0), axis=1)
    slot_of = jnp.sum(jnp.where(hit, line_slot[None], 0), axis=1)
    place = jnp.arange(NZ * 2, dtype=i32)
    col = jnp.arange(NZ * rows, dtype=i32)
    chosen = (turn[:, None, :] == (place % 2 + 1)[None, :, None]) & (
        (place // 2)[:, None] == (col // rows)[None, :]
    )[None]
    send_slots = jnp.sum(jnp.where(chosen, slot_of[:, None, :], 0), axis=2)
    send_rows = jnp.dot(
        chosen.astype(BF).reshape(NO * NZ * 2, NZ * rows), line_rows, preferred_element_type=F32
    ).astype(BF)
    send_slots = jnp.pad(send_slots, ((0, 0), (0, 128 - 2 * NZ))).reshape(NO, 1, 128)
    got_rows, got_slots, score = exchange(
        send_rows.reshape(NO, NZ * 2, width), send_slots, line_tokens, w, ws
    )
    got_rows = got_rows.reshape(NO * NZ * 2, width)
    got_slots = got_slots.reshape(NO, 128)[:, : 2 * NZ].reshape(NO * NZ * 2) - 1

    hidden = jax.nn.relu(jnp.dot(got_rows, class_in, preferred_element_type=F32)).astype(BF)
    all_logits = jnp.dot(hidden, class_out, preferred_element_type=F32)
    columns = jnp.arange(class_out.shape[1], dtype=i32)
    slot_logit = jnp.sum(jnp.where(got_slots[:, None] == columns[None, :], all_logits, 0.0), axis=1)
    bucket_end = jnp.cumsum(bucket_sizes.reshape(-1))
    positions = jnp.arange(passages.shape[0], dtype=i32)
    passage_bucket = jnp.sum((bucket_end[:, None] <= positions[None, :]).astype(i32), axis=0)
    similar = jnp.einsum("sd,pd->sp", got_rows, passages, preferred_element_type=F32)
    slot_mass = jnp.sum(
        jnp.where(got_slots[:, None] == passage_bucket[None, :], jnp.exp(similar), 0.0), axis=1
    )
    lane = jnp.arange(128, dtype=i32)
    logit3 = slot_logit.reshape(NO, NZ, 2)
    mass3 = slot_mass.reshape(NO, NZ, 2)
    odd = lane % 2 == 1
    spread = jnp.where(
        lane < 64,
        jnp.where(odd, logit3[:, :, 1:], logit3[:, :, :1]),
        jnp.where(odd, mass3[:, :, 1:], mass3[:, :, :1]),
    )
    ret = jnp.where((lane % 64) // 2 == mine, spread, 0.0)

    table, token_scores = give_back(ret, score)
    table = table.reshape(NZ, 128)
    logit_table = table[:, :64].reshape(NZ * 64)
    mass_table = table[:, 64:].reshape(NZ * 64)
    pick = code.reshape(-1)[:, None] == jnp.arange(NZ * 64, dtype=i32)[None, :]
    bucket_logit = jnp.sum(jnp.where(pick, logit_table[None], 0.0), axis=1).reshape(rows, top)
    bucket_mass = jnp.sum(jnp.where(pick, mass_table[None], 0.0), axis=1).reshape(rows, top)
    return (bucket_logit, bucket_mass, token_scores)


def solution(mesh):
    fine = Mesh(mesh.devices.reshape(NX, NZ, NC, NY), AXES)
    group = ("x", "z", "c")
    placed = (
        P(AXES, None),
        P(),
        P(None, AXES),
        P(AXES, None),
        P(AXES, None),
        P(AXES, None),
        P(AXES, None),
        P(group, "y"),
        P("y", group),
        P("y", group),
        P(group),
        P(),
    )
    return jax.shard_map(
        body,
        mesh=fine,
        in_specs=placed,
        out_specs=(P(AXES, None), P(AXES, None), P("y", None)),
        check_vma=False,
    )
```
